128 devices in a mesh: dp: 32 (over z, x, core), section: 4 (over y).
Axes of the slice: x: 4, y: 4, z: 4, core: 2. Of those that a mesh axis runs over, the one named last changes fastest.
Arguments:
- pair_grads: float32 [32, 4, 2, 1024, 256], P('dp', 'section'), may hold values from -80 to 80
- value_grads: float32 [32, 4, 1024, 1024], P('dp', 'section'), may hold values from -80 to 80
- pair_errors: float32 [32, 4, 2, 1024, 256], P('dp', 'section'), may hold values from -6 to 6
- value_errors: float32 [32, 4, 1024, 1024], P('dp', 'section'), may hold values from -6 to 6
- pair_basis: float32 [4, 2, 32, 256], P('section'), may hold values from -6 to 6
- value_basis: float32 [4, 32, 1024], P('section'), may hold values from -6 to 6
- pair_moment: float32 [4, 2, 1024, 256], P('section', None, 'dp'), may hold values from -6 to 6
- value_moment: float32 [4, 1024, 1024], P('section', 'dp'), may hold values from -6 to 6
- pair_weights: float32 [4, 2, 1024, 256], P('section', None, 'dp'), may hold values from -0.1875 to 0.1875
- value_weights: float32 [4, 1024, 1024], P('section', 'dp'), may hold values from -0.1875 to 0.1875
- gain_grads: float32 [32, 4, 2, 1024], P('dp', 'section'), may hold values from -6 to 6
- norm_gains: float32 [4, 2, 1024], P('section'), may hold values from 0.5 to 1.5
Outputs:
- pair_params: float32 [4, 2, 1024, 256], P('section', None, 'dp')
- value_params: float32 [4, 1024, 1024], P('section', 'dp')
- pair_velocity: float32 [4, 2, 1024, 256], P('section', None, 'dp')
- value_velocity: float32 [4, 1024, 1024], P('section', 'dp')
- gain_params: float32 [4, 2, 1024], P('section')
- pair_residue: float32 [32, 4, 2, 1024, 256], P('dp', 'section')
- value_residue: float32 [32, 4, 1024, 1024], P('dp', 'section')
- pair_factor: float32 [4, 2, 32, 256], P('section')
- value_factor: float32 [4, 32, 1024], P('section')
The draws below stay inside these ranges and needn't reach their ends.
All inputs are finite; a program needn't handle non-finite values.
Results may differ from the reference program's by a relative error of at most 0.00012.
Values sent between devices are 32-bit elements; how exact they have to be, the bound alone decides.
A program may use at most 128 MiB of HBM per device.

```python
import math
import jax
import jax.numpy as jnp
from jax import lax

D = 1024
QK = 256
R = 32
ROUNDS = 2
LAYERS = 4
N_DP = 32


def scaled_noise(key, salt, rows, cols):
    base = jax.random.fold_in(key, salt)
    row_scale = jnp.exp(jax.random.uniform(jax.random.fold_in(base, 1), (1, LAYERS, rows, 1), jnp.float32, math.log(0.3), math.log(3.0)))
    col_scale = jnp.exp(jax.random.uniform(jax.random.fold_in(base, 2), (1, LAYERS, rows, cols), jnp.float32, math.log(0.3), math.log(3.0))[:, :, :1, :])
    layer_scale = (0.5 + jnp.arange(LAYERS, dtype=jnp.float32) / max(LAYERS - 1, 1)).reshape(1, LAYERS, 1, 1)
    noise = jnp.clip(jax.random.normal(jax.random.fold_in(base, 3), (N_DP, LAYERS, rows, cols), jnp.float32), -4.0, 4.0)
    return noise * row_scale * col_scale * layer_scale


def draw_pair_grads(key, part):
    first = scaled_noise(key, 11, D, QK)
    second = scaled_noise(key, 12, D, QK)
    return jnp.stack([first, second], axis=2)


def draw_value_grads(key, part):
    return scaled_noise(key, 21, D, D)


def steps_of(own_key, dims, shards, low, largest):
    gain, own = 1.0, jax.random.fold_in(own_key, 6)
    for dim, shards_of in shards:
        draws = jnp.exp(jax.random.uniform(jax.random.fold_in(own, dim), (shards_of,), jnp.float32, low / len(shards), largest / len(shards)))
        gain = gain * jnp.repeat(draws, dims[dim] // shards_of).reshape([-1 if axis == dim else 1 for axis in range(len(dims))])
    return gain


def gaussian(key, extent, spread, bound, pieces=(), held_as=jnp.bfloat16):
    values = spread * jax.random.normal(key, extent, jnp.float32)
    if pieces:
        values = values * steps_of(key, extent, pieces, -0.22, 0.18)
    return jnp.clip(values, -bound, bound).astype(held_as)


def setup_inputs(seed: int = 0) -> dict:
    key_of = jax.random.split(jax.random.key(seed), 13)
    return {
        "pair_grads": draw_pair_grads(jax.random.fold_in(key_of[12], 71), 0),
        "value_grads": draw_value_grads(jax.random.fold_in(key_of[12], 71), 0),
        "pair_errors": gaussian(key_of[2], (N_DP, LAYERS, 2, D, QK), 1.0, 6.0, ((0, 32), (1, 4)), jnp.float32),
        "value_errors": gaussian(key_of[3], (N_DP, LAYERS, D, D), 1.0, 6.0, ((0, 32), (1, 4)), jnp.float32),
        "pair_basis": gaussian(key_of[4], (LAYERS, 2, R, QK), 1.0, 6.0, ((0, 4),), jnp.float32),
        "value_basis": gaussian(key_of[5], (LAYERS, R, D), 1.0, 6.0, ((0, 4),), jnp.float32),
        "pair_moment": gaussian(key_of[6], (LAYERS, 2, D, QK), 1.0, 6.0, ((0, 4), (2, 32)), jnp.float32),
        "value_moment": gaussian(key_of[7], (LAYERS, D, D), 1.0, 6.0, ((0, 4), (1, 32)), jnp.float32),
        "pair_weights": gaussian(key_of[8], (LAYERS, 2, D, QK), D ** -0.5, 0.1875, ((0, 4), (2, 32)), jnp.float32),
        "value_weights": gaussian(key_of[9], (LAYERS, D, D), D ** -0.5, 0.1875, ((0, 4), (1, 32)), jnp.float32),
        "gain_grads": gaussian(key_of[10], (N_DP, LAYERS, 2, D), 1.0, 6.0, ((0, 32), (1, 4)), jnp.float32),
        "norm_gains": jnp.clip(1.0 + 0.1 * jax.random.normal(key_of[11], (LAYERS, 2, D), jnp.float32), 0.5, 1.5),
    }


highest = lax.Precision.HIGHEST
momentum_rate = 0.9
step_rate = 0.3

def orthonormal(factor):
    gram = jnp.einsum('...rk,...sk->...rs', factor, factor, precision=highest)
    lower = jnp.linalg.cholesky(gram)
    return lax.linalg.triangular_solve(lower, factor, left_side=True, lower=True)

def power_rounds(full, basis):
    right = basis
    left_hat = None
    for step in range(ROUNDS):
        right_hat = orthonormal(right)
        left = jnp.einsum('rn,imn->rm', right_hat, full, precision=highest)
        left_hat = orthonormal(left)
        right = jnp.einsum('rm,imn->rn', left_hat, full, precision=highest)
    approx = jnp.dot(left_hat.T, right, precision=highest) / N_DP
    return (approx, right)

def reference(pair_grads, value_grads, pair_errors, value_errors, pair_basis, value_basis, pair_moment, value_moment, pair_weights, value_weights, gain_grads, norm_gains):
    pair_full = pair_grads + pair_errors
    value_full = value_grads + value_errors
    pair_list = []
    pair_rights = []
    value_list = []
    value_rights = []
    for layer in range(LAYERS):
        inner = []
        inner_right = []
        for which in range(2):
            approx, right = power_rounds(pair_full[:, layer, which], pair_basis[layer, which])
            inner.append(approx)
            inner_right.append(right)
        pair_list.append(jnp.stack(inner))
        pair_rights.append(jnp.stack(inner_right))
        approx, right = power_rounds(value_full[:, layer], value_basis[layer])
        value_list.append(approx)
        value_rights.append(right)
    pair_approx = jnp.stack(pair_list)
    value_approx = jnp.stack(value_list)
    pair_factor = jnp.stack(pair_rights)
    value_factor = jnp.stack(value_rights)
    pair_residue = pair_full - pair_approx[None]
    value_residue = value_full - value_approx[None]
    gain_mean = lax.optimization_barrier(jnp.sum(gain_grads, axis=0)) / N_DP
    total = jnp.sum(pair_approx * pair_approx) + jnp.sum(value_approx * value_approx) + jnp.sum(gain_mean * gain_mean)
    entries = LAYERS * (2 * D * QK + D * D + 2 * D)
    scale = 1.0 / jnp.sqrt(total / entries + 1e-06)
    pair_velocity = momentum_rate * pair_moment + scale * pair_approx
    value_velocity = momentum_rate * value_moment + scale * value_approx
    pair_params = pair_weights - step_rate * pair_velocity
    value_params = value_weights - step_rate * value_velocity
    gain_params = norm_gains - step_rate * scale * gain_mean
    return (pair_params, value_params, pair_velocity, value_velocity, gain_params, pair_residue, value_residue, pair_factor, value_factor)
```

```python
import jax
import jax.numpy as jnp
from jax import lax
from jax.experimental import pallas as pl
from jax.experimental.pallas import tpu as pltpu
from jax.sharding import PartitionSpec as P

MESH = pl.DeviceIdType.MESH
f32, bf16 = jnp.float32, jnp.bfloat16
NN = (((1,), (0,)), ((), ()))
NT = (((1,), (1,)), ((), ()))
highest = lax.Precision.HIGHEST

D, QK, R = 1024, 256, 32
N_DP, SECTIONS = 32, 4
SIDE = 4
CHIPS = SIDE * SIDE
TILE = 128
momentum_rate = 0.9
step_rate = 0.3

OFFSETS = ((2, 2), (2, 1), (2, 3), (1, 2), (3, 2), (0, 2), (2, 0), (1, 1), (1, 3), (3, 1), (3, 3), (0, 1), (0, 3), (1, 0), (3, 0))

PRODUCT, BULK, GAIN_PAIR, GAIN_ALL, GAIN_MEAN, LEFT, RIGHT, TOTAL = range(8, 16)


def split(a):
    high = a.astype(bf16)
    return high, (a - high.astype(f32)).astype(bf16)


def gram(a):
    return lax.dot_general(a, a, NT, precision=highest, preferred_element_type=f32)


def whiten(inverse, a):
    return lax.dot_general(inverse, a, NN, precision=highest, preferred_element_type=f32)


def inverse_factors(grams):
    row = lax.broadcasted_iota(jnp.int32, (R, 2 * R), 0)
    col = lax.broadcasted_iota(jnp.int32, (R, 2 * R), 1)
    eye = (row[:, :R] == col[:, :R]).astype(f32)

    def step(k, carry):
        out = []
        for both, pivots in carry:
            pivot_row = jnp.sum(jnp.where(row == k, both, 0.0), axis=0, keepdims=True)
            column = jnp.sum(jnp.where(col == k, both, 0.0), axis=1, keepdims=True)
            pivot = jnp.sum(jnp.where(col[:1] == k, pivot_row, 0.0), axis=1, keepdims=True)
            pivots = jnp.where(row[:, :1] == k, pivot, pivots)
            times = jnp.where(row[:, :1] > k, column / pivot, 0.0)
            out.append((both - times * pivot_row, pivots))
        return tuple(out)

    start = tuple((jnp.concatenate([g, eye], axis=1), jnp.zeros((R, 1), f32)) for g in grams)
    done = lax.fori_loop(0, R, step, start)
    return [both[:, R:] / jnp.sqrt(pivots) for both, pivots in done]


def load_tiles(ref, first, tiles):
    return jnp.concatenate([ref[(first + t) * R : (first + t + 1) * R, :] for t in range(tiles)], axis=1)


def store_tiles(ref, first, value):
    for t in range(value.shape[1] // TILE):
        ref[(first + t) * R : (first + t + 1) * R, :] = value[:, t * TILE : (t + 1) * TILE]


def product(factor, high, low, dims):
    both = jnp.concatenate(split(factor), axis=0)
    out = lax.dot_general(both, high, dims, preferred_element_type=f32)
    out = out + lax.dot_general(both, low, dims, preferred_element_type=f32)
    return out[:R] + out[R:]


def kernel(
    pg, vg, pe, ve, pbasis, vbasis, pmoment, vmoment, pweights, vweights, ggrads, gnorm,
    pparams, vparams, pvel, vvel, gparams, presidue, vresidue, pfactor, vfactor,
    ep, ev, pb, vb, pm, vm, pw, vw, gg, gn,
    p_own, v_own, p_in, v_in, p_other, v_other, ph, plow, vh, vlow,
    v_pay, v_rs, v_res, pl_pay, pl_rs, pl_res, pr_pay, pr_rs, pr_res,
    g_own, g_pair, g_send, g_in, g_mean,
    lhv, lhp, rv, rp, ltv, ltp, part, totals,
    load, send, recv,
):
    d = lax.axis_index("dp")
    s = lax.axis_index("section")
    c = d % 2
    chip = d // 2
    z, x = chip // SIDE, chip % SIDE

    def chip_at(dz, dx):
        return ((z + dz) % SIDE) * SIDE + (x + dx) % SIDE

    partner = (chip * 2 + 1 - c, s)
    line = tuple((dy, dc) for dy in (2, 1, 3, 0) for dc in (0, 1) if dy or dc)

    def on_line(dy, dc):
        return (chip * 2 + (c + dc) % 2, (s + dy) % SECTIONS)

    loads = []

    def start_load(source, target):
        copy = pltpu.make_async_copy(source, target, load.at[len(loads)])
        loads.append(copy)
        return copy

    basis_loads = [start_load(pbasis, pb), start_load(vbasis, vb)]
    pair_loads = [
        (w, r, start_load(pg.at[w, pl.ds(r, 512)], presidue.at[w, pl.ds(r, 512)]), start_load(pe.at[w, pl.ds(r, 512)], ep.at[w, pl.ds(r, 512)]))
        for w in range(2)
        for r in range(0, D, 512)
    ]
    value_loads = [
        (r, start_load(vg.at[pl.ds(r, 256)], vresidue.at[pl.ds(r, 256)]), start_load(ve.at[pl.ds(r, 256)], ev.at[pl.ds(r, 256)]))
        for r in range(0, D, 256)
    ]
    gain_load = start_load(ggrads, gg)
    late_loads = [start_load(pmoment, pm), start_load(vmoment, vm), start_load(pweights, pw), start_load(vweights, vw), start_load(gnorm, gn)]

    for copy in basis_loads:
        copy.start()

    @pl.when(c == 0)
    def _():
        for _, _, a, b in pair_loads:
            a.start()
            b.start()
        for _, a, b in value_loads:
            a.start()
            b.start()

    @pl.when(c == 1)
    def _():
        for _, a, b in value_loads:
            a.start()
            b.start()
        for _, _, a, b in pair_loads:
            a.start()
            b.start()

    gain_load.start()
    for copy in late_loads:
        copy.start()

    barrier = pltpu.get_barrier_semaphore()
    for dz, dx in OFFSETS:
        pl.semaphore_signal(barrier, inc=1, device_id=(chip_at(dz, dx) * 2 + c, s), device_id_type=MESH)
    for dy, dc in line:
        pl.semaphore_signal(barrier, inc=1, device_id=on_line(dy, dc), device_id_type=MESH)

    def put(source, target, slot, device):
        pltpu.make_async_remote_copy(
            src_ref=source, dst_ref=target, send_sem=send.at[slot], recv_sem=recv.at[slot], device_id=device, device_id_type=MESH
        ).start()

    def arrived(ref, slot):
        pltpu.make_async_copy(ref, ref, recv.at[slot]).wait()

    def gone(ref, slot):
        pltpu.make_async_copy(ref, ref, send.at[slot]).wait()

    for copy in basis_loads:
        copy.wait()

    def pair_stage(out):
        for w, r, a, b in pair_loads:
            a.wait()
            b.wait()
            full = presidue[w, r : r + 512, :] + ep[w, r : r + 512, :]
            presidue[w, r : r + 512, :] = full
            store_tiles(out, w * 8 + r // TILE, product(pb[w], *split(full), NT))

    def value_stage(out):
        for r, a, b in value_loads:
            a.wait()
            b.wait()
            full = vresidue[r : r + 256, :] + ev[r : r + 256, :]
            vresidue[r : r + 256, :] = full
            store_tiles(out, r // TILE, product(vb[...], *split(full), NT))

    def spread_gain(core):
        gain_load.wait()
        for w in range(2):
            for t in range(8):
                g_own[w, t : t + 1, :] = gg[w : w + 1, t * TILE : (t + 1) * TILE]
        put(g_own.at[1 - core], g_pair, GAIN_PAIR, partner)

    def sum_over_plane(index, pay, rs, res, rows, first=None, second=None):
        slot = 2 * index
        for k, (dz, dx) in enumerate(OFFSETS):
            other = chip_at(dz, dx)
            put(pay.at[pl.ds(pl.multiple_of(other * rows, 8), rows)], rs.at[k], slot, (other * 2 + c, s))
        if first is not None:
            first()
        arrived(rs, slot)
        own = pl.ds(pl.multiple_of(chip * rows, 8), rows)
        total = pay[own, :]
        for k in range(CHIPS - 1):
            total = total + rs[k]
        res[own, :] = total
        for dz, dx in OFFSETS:
            put(res.at[own], res.at[own], slot + 1, (chip_at(dz, dx) * 2 + c, s))
        if second is not None:
            second()
        rest = res.at[pl.ds(0, (CHIPS - 1) * rows)]
        arrived(rest, slot + 1)
        gone(rs, slot)
        gone(rest, slot + 1)

    def transposed(factor, out):
        high, low = split(factor)
        high, low = high.astype(f32), low.astype(f32)
        out[...] = jnp.concatenate([high, high, low], axis=0).T.astype(bf16)

    def right_stack(right):
        high, low = split(right * (1.0 / N_DP))
        return jnp.concatenate([high, low, high], axis=0)

    def rounds(core, left_bufs, right_bufs, count, right_tiles, bases, mats):
        left_pay, left_rs, left_res, left_rows = left_bufs
        right_pay, right_rs, right_res, right_rows = right_bufs
        state = {}

        def lefts(ref):
            return [load_tiles(ref, w * 8, 8) for w in range(count)]

        def rights(ref):
            return [load_tiles(ref, w * right_tiles, right_tiles) for w in range(count)]

        def first_wait():
            state["inverse"] = inverse_factors([gram(b) for b in bases()])

        def gains():
            arrived(g_pair, GAIN_PAIR)
            gone(g_pair, GAIN_PAIR)
            g_send[...] = g_own[core] + g_pair[...]

        def chip_sums():
            if core == 0:
                arrived(v_other, BULK)
                gone(p_other, BULK)
                for r in range(0, D, 128):
                    vh[r : r + 128, :], vlow[r : r + 128, :] = split(vresidue[r : r + 128, :] + v_other[r : r + 128, :])
            else:
                arrived(p_other, BULK)
                gone(v_other, BULK)
                for w in range(2):
                    for r in range(0, D, 256):
                        ph[w, r : r + 256, :], plow[w, r : r + 256, :] = split(presidue[w, r : r + 256, :] + p_other[w, r : r + 256, :])
            gains()

        def spread_gains():
            for k, (dz, dx) in enumerate(OFFSETS):
                put(g_send, g_in.at[k], GAIN_ALL, (chip_at(dz, dx) * 2 + c, s))

        def gain_means():
            arrived(g_in, GAIN_ALL)
            gone(g_in, GAIN_ALL)
            total = g_send[...]
            for k in range(CHIPS - 1):
                total = total + g_in[k]
            g_mean[core] = total / N_DP
            put(g_mean.at[core], g_mean.at[core], GAIN_MEAN, partner)

        for step in range(2):
            last = step == 1
            sum_over_plane(2 * step, left_pay[step], left_rs[step], left_res[step], left_rows, state.pop("overlap", first_wait), None if last else chip_sums)
            if not last:
                spread_gains()
            left = [whiten(i, a) for i, a in zip(state["inverse"], lefts(left_res[step]))]
            for w, a in enumerate(left):
                store_tiles(right_pay[step], w * right_tiles, product(a, *mats(w), NN))

            def factor_left():
                state["inverse"] = inverse_factors([gram(a) for a in left])
                if last:
                    for w, (i, a) in enumerate(zip(state["inverse"], left)):
                        hat = whiten(i, a)
                        if core == 0:
                            lhv[...] = hat
                        else:
                            lhp[w] = hat

            def after():
                if last:
                    if core == 0:
                        put(lhv, lhv, LEFT, partner)
                        transposed(lhv[...], ltv)
                        arrived(lhp, LEFT)
                        gone(lhv, LEFT)
                        for w in range(2):
                            transposed(lhp[w], ltp.at[w])
                    else:
                        put(lhp, lhp, LEFT, partner)
                        for w in range(2):
                            transposed(lhp[w], ltp.at[w])
                        arrived(lhv, LEFT)
                        gone(lhp, LEFT)
                        transposed(lhv[...], ltv)
                else:
                    gain_means()

            sum_over_plane(2 * step + 1, right_pay[step], right_rs[step], right_res[step], right_rows, factor_left, after)
            right = [whiten(i, a) for i, a in zip(state["inverse"], rights(right_res[step]))]
            if not last:
                for w, a in enumerate(right):
                    store_tiles(left_pay[1], w * 8, product(a, *mats(w), NT))

                def factor_right():
                    state["inverse"] = inverse_factors([gram(a) for a in right])

                state["overlap"] = factor_right
        return right

    def value_approx():
        stack = right_stack(rv[...])
        for r in range(0, D, 256):
            term = lax.dot_general(ltv[r : r + 256, :], stack, NN, preferred_element_type=f32)
            vresidue[r : r + 256, :] = vresidue[r : r + 256, :] - term
        vfactor[...] = rv[...]

    def pair_approx():
        for w in range(2):
            stack = right_stack(rp[w])
            for r in range(0, D, 512):
                term = lax.dot_general(ltp[w, r : r + 512, :], stack, NN, preferred_element_type=f32)
                presidue[w, r : r + 512, :] = presidue[w, r : r + 512, :] - term
            pfactor[w] = rp[w]

    def squares(terms):
        total = jnp.zeros((8, TILE), f32)
        for term in terms:
            term = term * term
            for r in range(0, term.shape[0], 8):
                for t in range(0, term.shape[1], TILE):
                    total = total + term[r : r + 8, t : t + TILE]
        return total

    def send_part(core, rights):
        part[...] = squares(rights) / (N_DP * N_DP) + squares([g_mean[core]])
        for k, (dy, dc) in enumerate(line):
            put(part, totals.at[k], TOTAL, on_line(dy, dc))

    @pl.when(c == 0)
    def _():
        pair_stage(pl_pay.at[0])
        pl.semaphore_wait(barrier, len(OFFSETS) + len(line))
        put(pl_pay.at[0], p_in, PRODUCT, partner)
        spread_gain(0)
        value_stage(v_own)
        put(presidue, p_other, BULK, partner)
        arrived(v_in, PRODUCT)
        v_pay[0] = v_own[...] + v_in[...]
        gone(p_in, PRODUCT)
        bufs = [v_pay.at[0], v_pay.at[1]], [v_rs.at[0], v_rs.at[1]], [v_res.at[0], v_res.at[1]], 16
        more = [v_pay.at[2], v_pay.at[3]], [v_rs.at[2], v_rs.at[3]], [v_res.at[2], v_res.at[3]], 16
        (right,) = rounds(0, bufs, more, 1, 8, lambda: [vb[...]], lambda w: (vh[...], vlow[...]))
        rv[...] = right
        put(rv, rv, RIGHT, partner)
        send_part(0, [right])
        value_approx()
        arrived(rp, RIGHT)
        pair_approx()
        gone(rv, RIGHT)

    @pl.when(c == 1)
    def _():
        value_stage(v_own)
        pl.semaphore_wait(barrier, len(OFFSETS) + len(line))
        put(v_own, v_in, PRODUCT, partner)
        spread_gain(1)
        pair_stage(p_own)
        put(vresidue, v_other, BULK, partner)
        arrived(p_in, PRODUCT)
        pl_pay[0] = p_own[...] + p_in[...]
        gone(v_in, PRODUCT)
        bufs = [pl_pay.at[0], pl_pay.at[1]], [pl_rs.at[0], pl_rs.at[1]], [pl_res.at[0], pl_res.at[1]], 32
        more = [pr_pay.at[0], pr_pay.at[1]], [pr_rs.at[0], pr_rs.at[1]], [pr_res.at[0], pr_res.at[1]], 8
        right = rounds(1, bufs, more, 2, 2, lambda: [pb[0], pb[1]], lambda w: (ph[w], plow[w]))
        for w in range(2):
            rp[w] = right[w]
        put(rp, rp, RIGHT, partner)
        send_part(1, right)
        pair_approx()
        arrived(rv, RIGHT)
        value_approx()
        gone(rp, RIGHT)

    for copy in late_loads:
        copy.wait()
    arrived(totals, TOTAL)
    gone(totals, TOTAL)
    arrived(g_mean.at[0], GAIN_MEAN)
    gone(g_mean.at[0], GAIN_MEAN)
    total = part[...]
    for k in range(len(line)):
        total = total + totals[k]
    total = jnp.sum(jnp.sum(total, axis=0, keepdims=True), axis=1, keepdims=True)
    entries = SECTIONS * (2 * D * QK + D * D + 2 * D)
    scale = 1.0 / jnp.sqrt(total / entries + 1e-06)
    rows = pl.ds(pl.multiple_of(d * R, R), R)
    term = lax.dot_general(ltv[rows, :], right_stack(rv[...]), NN, preferred_element_type=f32)
    velocity = momentum_rate * vm[...] + scale * term
    vvel[...] = velocity
    vparams[...] = vw[...] - step_rate * velocity
    for w in range(2):
        term = lax.dot_general(ltp[w, rows, :], right_stack(rp[w]), NN, preferred_element_type=f32)
        velocity = momentum_rate * pm[w] + scale * term
        pvel[w] = velocity
        pparams[w] = pw[w] - step_rate * velocity
        for t in range(8):
            at = slice(t * TILE, (t + 1) * TILE)
            gparams[w : w + 1, at] = gn[w : w + 1, at] - step_rate * scale * g_mean[w, t : t + 1, :]


def local(
    pair_grads, value_grads, pair_errors, value_errors, pair_basis, value_basis,
    pair_moment, value_moment, pair_weights, value_weights, gain_grads, norm_gains,
):
    any_space = pl.BlockSpec(memory_space=pl.ANY)
    vmem = pl.BlockSpec(memory_space=pltpu.VMEM)

    def shape(*dims):
        return jax.ShapeDtypeStruct(dims, f32)

    def scratch(*dims, dtype=f32):
        return pltpu.VMEM(dims, dtype)

    out = pl.pallas_call(
        kernel,
        name="power_rounds",
        out_shape=(
            shape(2, R, QK), shape(R, D), shape(2, R, QK), shape(R, D), shape(2, D),
            shape(2, D, QK), shape(D, D), shape(2, R, QK), shape(R, D),
        ),
        in_specs=[any_space] * 12,
        out_specs=(vmem,) * 9,
        scratch_shapes=[
            scratch(2, D, QK), scratch(D, D), scratch(2, R, QK), scratch(R, D),
            scratch(2, R, QK), scratch(R, D), scratch(2, R, QK), scratch(R, D), scratch(2, D), scratch(2, D),
            scratch(512, TILE), scratch(256, TILE), scratch(512, TILE), scratch(256, TILE),
            scratch(2, D, QK), scratch(D, D),
            scratch(2, D, QK, dtype=bf16), scratch(2, D, QK, dtype=bf16), scratch(D, D, dtype=bf16), scratch(D, D, dtype=bf16),
            scratch(4, 256, TILE), scratch(4, 15, 16, TILE), scratch(4, 256, TILE),
            scratch(2, 512, TILE), scratch(2, 15, 32, TILE), scratch(2, 512, TILE),
            scratch(2, 128, TILE), scratch(2, 15, 8, TILE), scratch(2, 128, TILE),
            scratch(2, 8, TILE), scratch(8, TILE), scratch(8, TILE), scratch(15, 8, TILE), scratch(2, 8, TILE),
            scratch(R, D), scratch(2, R, D), scratch(R, D), scratch(2, R, QK),
            scratch(D, 3 * R, dtype=bf16), scratch(2, D, 3 * R, dtype=bf16),
            scratch(8, TILE), scratch(7, 8, TILE),
            pltpu.SemaphoreType.DMA((24,)), pltpu.SemaphoreType.DMA((16,)), pltpu.SemaphoreType.DMA((16,)),
        ],
        compiler_params=pltpu.CompilerParams(collective_id=0, has_side_effects=True, vmem_limit_bytes=48 * 1024 * 1024),
    )(
        pair_grads[0, 0], value_grads[0, 0], pair_errors[0, 0], value_errors[0, 0], pair_basis[0], value_basis[0],
        pair_moment[0], value_moment[0], pair_weights[0], value_weights[0], gain_grads[0, 0], norm_gains[0],
    )
    pparams, vparams, pvel, vvel, gparams, presidue, vresidue, pfactor, vfactor = out
    return (
        pparams[None], vparams[None], pvel[None], vvel[None], gparams[None],
        presidue[None, None], vresidue[None, None], pfactor[None], vfactor[None],
    )


def solution(mesh):
    in_specs = (
        P("dp", "section", None, None, None),
        P("dp", "section", None, None),
        P("dp", "section", None, None, None),
        P("dp", "section", None, None),
        P("section", None, None, None),
        P("section", None, None),
        P("section", None, "dp", None),
        P("section", "dp", None),
        P("section", None, "dp", None),
        P("section", "dp", None),
        P("dp", "section", None, None),
        P("section", None, None),
    )
    out_specs = (
        P("section", None, "dp", None),
        P("section", "dp", None),
        P("section", None, "dp", None),
        P("section", "dp", None),
        P("section", None, None),
        P("dp", "section", None, None, None),
        P("dp", "section", None, None),
        P("section", None, None, None),
        P("section", None, None),
    )
    return jax.shard_map(local, mesh=mesh, in_specs=in_specs, out_specs=out_specs, check_vma=False)
```

```python
import jax
import jax.numpy as jnp
from jax import lax
from jax.experimental import pallas as pl
from jax.experimental.pallas import tpu as pltpu
from jax.sharding import PartitionSpec as P

MESH = pl.DeviceIdType.MESH
f32, bf16 = jnp.float32, jnp.bfloat16
NN = (((1,), (0,)), ((), ()))
NT = (((1,), (1,)), ((), ()))
highest = lax.Precision.HIGHEST

D, QK, R = 1024, 256, 32
N_DP, SECTIONS = 32, 4
SIDE = 4
CHIPS = SIDE * SIDE
TILE = 128
momentum_rate = 0.9
step_rate = 0.3

OFFSETS = ((2, 2), (2, 1), (2, 3), (1, 2), (3, 2), (0, 2), (2, 0), (1, 1), (1, 3), (3, 1), (3, 3), (0, 1), (0, 3), (1, 0), (3, 0))

PRODUCT, BULK, GAIN_PAIR, GAIN_ALL, GAIN_MEAN, LEFT, RIGHT, TOTAL = range(8, 16)


def split(a):
    high = a.astype(bf16)
    return high, (a - high.astype(f32)).astype(bf16)


def gram(a):
    return lax.dot_general(a, a, NT, precision=highest, preferred_element_type=f32)


def whiten(inverse, a):
    return lax.dot_general(inverse, a, NN, precision=highest, preferred_element_type=f32)


def inverse_factors(grams):
    row = lax.broadcasted_iota(jnp.int32, (R, 2 * R), 0)
    col = lax.broadcasted_iota(jnp.int32, (R, 2 * R), 1)
    eye = (row[:, :R] == col[:, :R]).astype(f32)

    def step(k, carry):
        out = []
        for both, pivots in carry:
            pivot_row = jnp.sum(jnp.where(row == k, both, 0.0), axis=0, keepdims=True)
            column = jnp.sum(jnp.where(col == k, both, 0.0), axis=1, keepdims=True)
            pivot = jnp.sum(jnp.where(col[:1] == k, pivot_row, 0.0), axis=1, keepdims=True)
            pivots = jnp.where(row[:, :1] == k, pivot, pivots)
            times = jnp.where(row[:, :1] > k, column / pivot, 0.0)
            out.append((both - times * pivot_row, pivots))
        return tuple(out)

    start = tuple((jnp.concatenate([g, eye], axis=1), jnp.zeros((R, 1), f32)) for g in grams)
    done = lax.fori_loop(0, R, step, start)
    return [both[:, R:] / jnp.sqrt(pivots) for both, pivots in done]


def load_tiles(ref, first, tiles):
    return jnp.concatenate([ref[(first + t) * R : (first + t + 1) * R, :] for t in range(tiles)], axis=1)


def store_tiles(ref, first, value):
    for t in range(value.shape[1] // TILE):
        ref[(first + t) * R : (first + t + 1) * R, :] = value[:, t * TILE : (t + 1) * TILE]


def product(factor, high, low, dims):
    both = jnp.concatenate(split(factor), axis=0)
    out = lax.dot_general(both, high, dims, preferred_element_type=f32)
    out = out + lax.dot_general(both, low, dims, preferred_element_type=f32)
    return out[:R] + out[R:]


def kernel(
    pg, vg, pe, ve, pbasis, vbasis, pmoment, vmoment, pweights, vweights, ggrads, gnorm,
    pparams, vparams, pvel, vvel, gparams, presidue, vresidue, pfactor, vfactor,
    ep, ev, pb, vb, pm, vm, pw, vw, gg, gn,
    p_own, v_own, p_in, v_in, p_other, v_other, ph, plow, vh, vlow,
    v_pay, v_rs, v_res, pl_pay, pl_rs, pl_res, pr_pay, pr_rs, pr_res,
    g_own, g_pair, g_send, g_in, g_mean,
    lhv, lhp, rv, rp, ltv, ltp, part, totals,
    load, send, recv,
):
    d = lax.axis_index("dp")
    s = lax.axis_index("section")
    c = d % 2
    chip = d // 2
    z, x = chip // SIDE, chip % SIDE

    def chip_at(dz, dx):
        return ((z + dz) % SIDE) * SIDE + (x + dx) % SIDE

    partner = (chip * 2 + 1 - c, s)
    line = tuple((dy, dc) for dy in (2, 1, 3, 0) for dc in (0, 1) if dy or dc)

    def on_line(dy, dc):
        return (chip * 2 + (c + dc) % 2, (s + dy) % SECTIONS)

    loads = []

    def start_load(source, target):
        copy = pltpu.make_async_copy(source, target, load.at[len(loads)])
        loads.append(copy)
        return copy

    basis_loads = [start_load(pbasis, pb), start_load(vbasis, vb)]
    pair_loads = [
        (w, r, start_load(pg.at[w, pl.ds(r, 512)], presidue.at[w, pl.ds(r, 512)]), start_load(pe.at[w, pl.ds(r, 512)], ep.at[w, pl.ds(r, 512)]))
        for w in range(2)
        for r in range(0, D, 512)
    ]
    value_loads = [
        (r, start_load(vg.at[pl.ds(r, 256)], vresidue.at[pl.ds(r, 256)]), start_load(ve.at[pl.ds(r, 256)], ev.at[pl.ds(r, 256)]))
        for r in range(0, D, 256)
    ]
    gain_load = start_load(ggrads, gg)
    late_loads = [start_load(pmoment, pm), start_load(vmoment, vm), start_load(pweights, pw), start_load(vweights, vw), start_load(gnorm, gn)]

    for copy in basis_loads:
        copy.start()

    @pl.when(c == 0)
    def _():
        for _, _, a, b in pair_loads:
            a.start()
            b.start()
        for _, a, b in value_loads:
            a.start()
            b.start()

    @pl.when(c == 1)
    def _():
        for _, a, b in value_loads:
            a.start()
            b.start()
        for _, _, a, b in pair_loads:
            a.start()
            b.start()

    gain_load.start()
    for copy in late_loads:
        copy.start()

    barrier = pltpu.get_barrier_semaphore()
    for dz, dx in OFFSETS:
        pl.semaphore_signal(barrier, inc=1, device_id=(chip_at(dz, dx) * 2 + c, s), device_id_type=MESH)
    for dy, dc in line:
        pl.semaphore_signal(barrier, inc=1, device_id=on_line(dy, dc), device_id_type=MESH)

    def put(source, target, slot, device):
        pltpu.make_async_remote_copy(
            src_ref=source, dst_ref=target, send_sem=send.at[slot], recv_sem=recv.at[slot], device_id=device, device_id_type=MESH
        ).start()

    def arrived(ref, slot):
        pltpu.make_async_copy(ref, ref, recv.at[slot]).wait()

    def gone(ref, slot):
        pltpu.make_async_copy(ref, ref, send.at[slot]).wait()

    for copy in basis_loads:
        copy.wait()

    def pair_stage(out, part=slice(None)):
        for w, r, a, b in pair_loads[part]:
            a.wait()
            b.wait()
            full = presidue[w, r : r + 512, :] + ep[w, r : r + 512, :]
            presidue[w, r : r + 512, :] = full
            store_tiles(out, w * 8 + r // TILE, product(pb[w], *split(full), NT))

    def value_stage(out, part=slice(None)):
        for r, a, b in value_loads[part]:
            a.wait()
            b.wait()
            full = vresidue[r : r + 256, :] + ev[r : r + 256, :]
            vresidue[r : r + 256, :] = full
            store_tiles(out, r // TILE, product(vb[...], *split(full), NT))

    def spread_gain(core):
        gain_load.wait()
        for w in range(2):
            for t in range(8):
                g_own[w, t : t + 1, :] = gg[w : w + 1, t * TILE : (t + 1) * TILE]
        put(g_own.at[1 - core], g_pair, GAIN_PAIR, partner)

    def sum_over_plane(index, pay, rs, res, rows, first=None, second=None):
        slot = 2 * index
        for k, (dz, dx) in enumerate(OFFSETS):
            other = chip_at(dz, dx)
            put(pay.at[pl.ds(pl.multiple_of(other * rows, 8), rows)], rs.at[k], slot, (other * 2 + c, s))
        if first is not None:
            first()
        arrived(rs, slot)
        own = pl.ds(pl.multiple_of(chip * rows, 8), rows)
        total = pay[own, :]
        for k in range(CHIPS - 1):
            total = total + rs[k]
        res[own, :] = total
        for dz, dx in OFFSETS:
            put(res.at[own], res.at[own], slot + 1, (chip_at(dz, dx) * 2 + c, s))
        if second is not None:
            second()
        rest = res.at[pl.ds(0, (CHIPS - 1) * rows)]
        arrived(rest, slot + 1)
        gone(rs, slot)
        gone(rest, slot + 1)

    def transposed(factor, out):
        high, low = split(factor)
        high, low = high.astype(f32), low.astype(f32)
        out[...] = jnp.concatenate([high, high, low], axis=0).T.astype(bf16)

    def right_stack(right):
        high, low = split(right * (1.0 / N_DP))
        return jnp.concatenate([high, low, high], axis=0)

    def rounds(core, left_bufs, right_bufs, count, right_tiles, bases, mats):
        left_pay, left_rs, left_res, left_rows = left_bufs
        right_pay, right_rs, right_res, right_rows = right_bufs
        state = {}

        def lefts(ref):
            return [load_tiles(ref, w * 8, 8) for w in range(count)]

        def rights(ref):
            return [load_tiles(ref, w * right_tiles, right_tiles) for w in range(count)]

        def first_wait():
            if core == 0:
                put(presidue, p_other, BULK, partner)
            else:
                put(vresidue, v_other, BULK, partner)
            state["inverse"] = inverse_factors([gram(b) for b in bases()])

        def gains():
            arrived(g_pair, GAIN_PAIR)
            gone(g_pair, GAIN_PAIR)
            g_send[...] = g_own[core] + g_pair[...]

        def chip_sums():
            if core == 0:
                arrived(v_other, BULK)
                gone(p_other, BULK)
                for r in range(0, D, 128):
                    vh[r : r + 128, :], vlow[r : r + 128, :] = split(vresidue[r : r + 128, :] + v_other[r : r + 128, :])
            else:
                arrived(p_other, BULK)
                gone(v_other, BULK)
                for w in range(2):
                    for r in range(0, D, 256):
                        ph[w, r : r + 256, :], plow[w, r : r + 256, :] = split(presidue[w, r : r + 256, :] + p_other[w, r : r + 256, :])
            gains()

        def spread_gains():
            for k, (dz, dx) in enumerate(OFFSETS):
                put(g_send, g_in.at[k], GAIN_ALL, (chip_at(dz, dx) * 2 + c, s))

        def gain_means():
            arrived(g_in, GAIN_ALL)
            gone(g_in, GAIN_ALL)
            total = g_send[...]
            for k in range(CHIPS - 1):
                total = total + g_in[k]
            g_mean[core] = total / N_DP
            put(g_mean.at[core], g_mean.at[core], GAIN_MEAN, partner)

        for step in range(2):
            last = step == 1
            sum_over_plane(2 * step, left_pay[step], left_rs[step], left_res[step], left_rows, state.pop("overlap", first_wait), None if last else chip_sums)
            left = [whiten(i, a) for i, a in zip(state["inverse"], lefts(left_res[step]))]
            for w, a in enumerate(left):
                store_tiles(right_pay[step], w * right_tiles, product(a, *mats(w), NN))

            def factor_left():
                state["inverse"] = inverse_factors([gram(a) for a in left])
                if last:
                    for w, (i, a) in enumerate(zip(state["inverse"], left)):
                        hat = whiten(i, a)
                        if core == 0:
                            lhv[...] = hat
                        else:
                            lhp[w] = hat
                else:
                    spread_gains()

            def after():
                if last:
                    if core == 0:
                        put(lhv, lhv, LEFT, partner)
                        transposed(lhv[...], ltv)
                        arrived(lhp, LEFT)
                        gone(lhv, LEFT)
                        for w in range(2):
                            transposed(lhp[w], ltp.at[w])
                    else:
                        put(lhp, lhp, LEFT, partner)
                        for w in range(2):
                            transposed(lhp[w], ltp.at[w])
                        arrived(lhv, LEFT)
                        gone(lhp, LEFT)
                        transposed(lhv[...], ltv)
                else:
                    gain_means()

            sum_over_plane(2 * step + 1, right_pay[step], right_rs[step], right_res[step], right_rows, factor_left, after)
            right = [whiten(i, a) for i, a in zip(state["inverse"], rights(right_res[step]))]
            if not last:
                for w, a in enumerate(right):
                    store_tiles(left_pay[1], w * 8, product(a, *mats(w), NT))

                def factor_right():
                    state["inverse"] = inverse_factors([gram(a) for a in right])

                state["overlap"] = factor_right
        return right

    def value_approx():
        stack = right_stack(rv[...])
        for r in range(0, D, 256):
            term = lax.dot_general(ltv[r : r + 256, :], stack, NN, preferred_element_type=f32)
            vresidue[r : r + 256, :] = vresidue[r : r + 256, :] - term
        vfactor[...] = rv[...]

    def pair_approx():
        for w in range(2):
            stack = right_stack(rp[w])
            for r in range(0, D, 512):
                term = lax.dot_general(ltp[w, r : r + 512, :], stack, NN, preferred_element_type=f32)
                presidue[w, r : r + 512, :] = presidue[w, r : r + 512, :] - term
            pfactor[w] = rp[w]

    def squares(terms):
        total = jnp.zeros((8, TILE), f32)
        for term in terms:
            term = term * term
            for r in range(0, term.shape[0], 8):
                for t in range(0, term.shape[1], TILE):
                    total = total + term[r : r + 8, t : t + TILE]
        return total

    def send_part(core, rights):
        part[...] = squares(rights) / (N_DP * N_DP) + squares([g_mean[core]])
        for k, (dy, dc) in enumerate(line):
            put(part, totals.at[k], TOTAL, on_line(dy, dc))

    @pl.when(c == 0)
    def _():
        pair_stage(pl_pay.at[0])
        value_stage(v_own, slice(0, 2))
        pl.semaphore_wait(barrier, len(OFFSETS) + len(line))
        put(pl_pay.at[0], p_in, PRODUCT, partner)
        spread_gain(0)
        value_stage(v_own, slice(2, 4))
        arrived(v_in, PRODUCT)
        v_pay[0] = v_own[...] + v_in[...]
        gone(p_in, PRODUCT)
        bufs = [v_pay.at[0], v_pay.at[1]], [v_rs.at[0], v_rs.at[1]], [v_res.at[0], v_res.at[1]], 16
        more = [v_pay.at[2], v_pay.at[3]], [v_rs.at[2], v_rs.at[3]], [v_res.at[2], v_res.at[3]], 16
        (right,) = rounds(0, bufs, more, 1, 8, lambda: [vb[...]], lambda w: (vh[...], vlow[...]))
        rv[...] = right
        put(rv, rv, RIGHT, partner)
        send_part(0, [right])
        value_approx()
        arrived(rp, RIGHT)
        pair_approx()
        gone(rv, RIGHT)

    @pl.when(c == 1)
    def _():
        value_stage(v_own)
        pair_stage(p_own, slice(0, 2))
        pl.semaphore_wait(barrier, len(OFFSETS) + len(line))
        put(v_own, v_in, PRODUCT, partner)
        spread_gain(1)
        pair_stage(p_own, slice(2, 4))
        arrived(p_in, PRODUCT)
        pl_pay[0] = p_own[...] + p_in[...]
        gone(v_in, PRODUCT)
        bufs = [pl_pay.at[0], pl_pay.at[1]], [pl_rs.at[0], pl_rs.at[1]], [pl_res.at[0], pl_res.at[1]], 32
        more = [pr_pay.at[0], pr_pay.at[1]], [pr_rs.at[0], pr_rs.at[1]], [pr_res.at[0], pr_res.at[1]], 8
        right = rounds(1, bufs, more, 2, 2, lambda: [pb[0], pb[1]], lambda w: (ph[w], plow[w]))
        for w in range(2):
            rp[w] = right[w]
        put(rp, rp, RIGHT, partner)
        send_part(1, right)
        pair_approx()
        arrived(rv, RIGHT)
        value_approx()
        gone(rp, RIGHT)

    for copy in late_loads:
        copy.wait()
    arrived(g_mean.at[0], GAIN_MEAN)
    gone(g_mean.at[0], GAIN_MEAN)
    rows = pl.ds(pl.multiple_of(d * R, R), R)
    vterm = lax.dot_general(ltv[rows, :], right_stack(rv[...]), NN, preferred_element_type=f32)
    pterms = [lax.dot_general(ltp[w, rows, :], right_stack(rp[w]), NN, preferred_element_type=f32) for w in range(2)]
    rv[...] = vterm
    for w in range(2):
        rp[w] = pterms[w]
    arrived(totals, TOTAL)
    gone(totals, TOTAL)
    total = part[...]
    for k in range(len(line)):
        total = total + totals[k]
    total = jnp.sum(jnp.sum(total, axis=0, keepdims=True), axis=1, keepdims=True)
    entries = SECTIONS * (2 * D * QK + D * D + 2 * D)
    scale = 1.0 / jnp.sqrt(total / entries + 1e-06)
    velocity = momentum_rate * vm[...] + scale * rv[...]
    vvel[...] = velocity
    vparams[...] = vw[...] - step_rate * velocity
    for w in range(2):
        velocity = momentum_rate * pm[w] + scale * rp[w]
        pvel[w] = velocity
        pparams[w] = pw[w] - step_rate * velocity
        for t in range(8):
            at = slice(t * TILE, (t + 1) * TILE)
            gparams[w : w + 1, at] = gn[w : w + 1, at] - step_rate * scale * g_mean[w, t : t + 1, :]


def write_out(*refs):
    count = len(refs) // 2
    sems = refs[-1]
    copies = [pltpu.make_async_copy(refs[i], refs[count + i], sems.at[i]) for i in (6, 5, 0, 1, 2, 3, 4, 7, 8)]
    for copy in copies:
        copy.start()
    for copy in copies:
        copy.wait()


def local(
    pair_grads, value_grads, pair_errors, value_errors, pair_basis, value_basis,
    pair_moment, value_moment, pair_weights, value_weights, gain_grads, norm_gains,
):
    any_space = pl.BlockSpec(memory_space=pltpu.HBM)
    vmem = pl.BlockSpec(memory_space=pltpu.VMEM)

    def shape(*dims):
        return jax.ShapeDtypeStruct(dims, f32)

    def scratch(*dims, dtype=f32):
        return pltpu.VMEM(dims, dtype)

    out = pl.pallas_call(
        kernel,
        name="power_rounds",
        out_shape=(
            shape(2, R, QK), shape(R, D), shape(2, R, QK), shape(R, D), shape(2, D),
            shape(2, D, QK), shape(D, D), shape(2, R, QK), shape(R, D),
        ),
        in_specs=[any_space] * 12,
        out_specs=(vmem,) * 9,
        scratch_shapes=[
            scratch(2, D, QK), scratch(D, D), scratch(2, R, QK), scratch(R, D),
            scratch(2, R, QK), scratch(R, D), scratch(2, R, QK), scratch(R, D), scratch(2, D), scratch(2, D),
            scratch(512, TILE), scratch(256, TILE), scratch(512, TILE), scratch(256, TILE),
            scratch(2, D, QK), scratch(D, D),
            scratch(2, D, QK, dtype=bf16), scratch(2, D, QK, dtype=bf16), scratch(D, D, dtype=bf16), scratch(D, D, dtype=bf16),
            scratch(4, 256, TILE), scratch(4, 15, 16, TILE), scratch(4, 256, TILE),
            scratch(2, 512, TILE), scratch(2, 15, 32, TILE), scratch(2, 512, TILE),
            scratch(2, 128, TILE), scratch(2, 15, 8, TILE), scratch(2, 128, TILE),
            scratch(2, 8, TILE), scratch(8, TILE), scratch(8, TILE), scratch(15, 8, TILE), scratch(2, 8, TILE),
            scratch(R, D), scratch(2, R, D), scratch(R, D), scratch(2, R, QK),
            scratch(D, 3 * R, dtype=bf16), scratch(2, D, 3 * R, dtype=bf16),
            scratch(8, TILE), scratch(7, 8, TILE),
            pltpu.SemaphoreType.DMA((24,)), pltpu.SemaphoreType.DMA((16,)), pltpu.SemaphoreType.DMA((16,)),
        ],
        compiler_params=pltpu.CompilerParams(collective_id=0, has_side_effects=True, vmem_limit_bytes=36 * 1024 * 1024),
    )(*(pltpu.with_memory_space_constraint(a, pltpu.HBM) for a in (
        pair_grads[0, 0], value_grads[0, 0], pair_errors[0, 0], value_errors[0, 0], pair_basis[0], value_basis[0],
        pair_moment[0], value_moment[0], pair_weights[0], value_weights[0], gain_grads[0, 0], norm_gains[0],
    )))
    out = pl.pallas_call(
        write_out,
        name="write_out",
        out_shape=tuple(jax.ShapeDtypeStruct(a.shape, f32) for a in out),
        in_specs=[vmem] * 9,
        out_specs=(pl.BlockSpec(memory_space=pltpu.HBM),) * 9,
        scratch_shapes=[pltpu.SemaphoreType.DMA((9,))],
        compiler_params=pltpu.CompilerParams(vmem_limit_bytes=16 * 1024 * 1024),
    )(*out)
    pparams, vparams, pvel, vvel, gparams, presidue, vresidue, pfactor, vfactor = out
    return (
        pparams[None], vparams[None], pvel[None], vvel[None], gparams[None],
        presidue[None, None], vresidue[None, None], pfactor[None], vfactor[None],
    )


def solution(mesh):
    in_specs = (
        P("dp", "section", None, None, None),
        P("dp", "section", None, None),
        P("dp", "section", None, None, None),
        P("dp", "section", None, None),
        P("section", None, None, None),
        P("section", None, None),
        P("section", None, "dp", None),
        P("section", "dp", None),
        P("section", None, "dp", None),
        P("section", "dp", None),
        P("dp", "section", None, None),
        P("section", None, None),
    )
    out_specs = (
        P("section", None, "dp", None),
        P("section", "dp", None),
        P("section", None, "dp", None),
        P("section", "dp", None),
        P("section", None, None),
        P("dp", "section", None, None, None),
        P("dp", "section", None, None),
        P("section", None, None, None),
        P("section", None, None),
    )
    return jax.shard_map(local, mesh=mesh, in_specs=in_specs, out_specs=out_specs, check_vma=False)
```

```python
import jax
import jax.numpy as jnp
from jax import lax
from jax.experimental import pallas as pl
from jax.experimental.pallas import tpu as pltpu
from jax.sharding import PartitionSpec as P

MESH = pl.DeviceIdType.MESH
f32, bf16 = jnp.float32, jnp.bfloat16
NN = (((1,), (0,)), ((), ()))
NT = (((1,), (1,)), ((), ()))
highest = lax.Precision.HIGHEST

D, QK, R = 1024, 256, 32
N_DP, SECTIONS = 32, 4
SIDE = 4
CHIPS = SIDE * SIDE
TILE = 128
momentum_rate = 0.9
step_rate = 0.3

OFFSETS = ((2, 2), (2, 1), (2, 3), (1, 2), (3, 2), (0, 2), (2, 0), (1, 1), (1, 3), (3, 1), (3, 3), (0, 1), (0, 3), (1, 0), (3, 0))

PRODUCT, BULK, GAIN_PAIR, GAIN_ALL, GAIN_MEAN, LEFT, RIGHT, TOTAL = range(8, 16)


def split(a):
    high = a.astype(bf16)
    return high, (a - high.astype(f32)).astype(bf16)


def gram(a):
    return lax.dot_general(a, a, NT, precision=highest, preferred_element_type=f32)


def whiten(inverse, a):
    return lax.dot_general(inverse, a, NN, precision=highest, preferred_element_type=f32)


def inverse_factors(grams):
    row = lax.broadcasted_iota(jnp.int32, (R, 2 * R), 0)
    col = lax.broadcasted_iota(jnp.int32, (R, 2 * R), 1)
    eye = (row[:, :R] == col[:, :R]).astype(f32)

    def step(k, carry):
        out = []
        for both, pivots in carry:
            pivot_row = jnp.sum(jnp.where(row == k, both, 0.0), axis=0, keepdims=True)
            column = jnp.sum(jnp.where(col == k, both, 0.0), axis=1, keepdims=True)
            pivot = jnp.sum(jnp.where(col[:1] == k, pivot_row, 0.0), axis=1, keepdims=True)
            pivots = jnp.where(row[:, :1] == k, pivot, pivots)
            times = jnp.where(row[:, :1] > k, column / pivot, 0.0)
            out.append((both - times * pivot_row, pivots))
        return tuple(out)

    start = tuple((jnp.concatenate([g, eye], axis=1), jnp.zeros((R, 1), f32)) for g in grams)
    done = lax.fori_loop(0, R, step, start)
    return [both[:, R:] / jnp.sqrt(pivots) for both, pivots in done]


def load_tiles(ref, first, tiles):
    return jnp.concatenate([ref[(first + t) * R : (first + t + 1) * R, :] for t in range(tiles)], axis=1)


def store_tiles(ref, first, value):
    for t in range(value.shape[1] // TILE):
        ref[(first + t) * R : (first + t + 1) * R, :] = value[:, t * TILE : (t + 1) * TILE]


def product(factor, high, low, dims):
    both = jnp.concatenate(split(factor), axis=0)
    out = lax.dot_general(both, high, dims, preferred_element_type=f32)
    out = out + lax.dot_general(both, low, dims, preferred_element_type=f32)
    return out[:R] + out[R:]


def kernel(
    pg, vg, pe, ve, pbasis, vbasis, pmoment, vmoment, pweights, vweights, ggrads, gnorm,
    pparams, vparams, pvel, vvel, gparams, presidue, vresidue, pfactor, vfactor,
    ep, ev, pb, vb, pm, vm, pw, vw, gg, gn,
    p_own, v_own, p_in, v_in, p_other, v_other, ph, plow, vh, vlow, pth, ptlow, vth, vtlow,
    v_pay, v_rs, v_res, pl_pay, pl_rs, pl_res,
    vr_pay, vr_in, vr_mid, vr_next, vr_res, pr_pay, pr_in, pr_mid, pr_next, pr_res,
    g_own, g_pair, g_send, g_in, g_mean,
    lhv, lhp, rv, rp, ltv, ltp, part, totals,
    load, send, recv,
):
    d = lax.axis_index("dp")
    s = lax.axis_index("section")
    c = d % 2
    chip = d // 2
    z, x = chip // SIDE, chip % SIDE

    def chip_at(dz, dx):
        return ((z + dz) % SIDE) * SIDE + (x + dx) % SIDE

    partner = (chip * 2 + 1 - c, s)
    line = tuple((dy, dc) for dy in (2, 1, 3, 0) for dc in (0, 1) if dy or dc)

    def on_line(dy, dc):
        return (chip * 2 + (c + dc) % 2, (s + dy) % SECTIONS)

    loads = []

    def start_load(source, target):
        copy = pltpu.make_async_copy(source, target, load.at[len(loads)])
        loads.append(copy)
        return copy

    basis_loads = [start_load(pbasis, pb), start_load(vbasis, vb)]
    pair_loads = [
        (w, r, start_load(pg.at[w, pl.ds(r, 512)], presidue.at[w, pl.ds(r, 512)]), start_load(pe.at[w, pl.ds(r, 512)], ep.at[w, pl.ds(r, 512)]))
        for w in range(2)
        for r in range(0, D, 512)
    ]
    value_loads = [
        (r, start_load(vg.at[pl.ds(r, 256)], vresidue.at[pl.ds(r, 256)]), start_load(ve.at[pl.ds(r, 256)], ev.at[pl.ds(r, 256)]))
        for r in range(0, D, 256)
    ]
    gain_load = start_load(ggrads, gg)
    late_loads = [start_load(pmoment, pm), start_load(vmoment, vm), start_load(pweights, pw), start_load(vweights, vw), start_load(gnorm, gn)]

    for copy in basis_loads:
        copy.start()

    @pl.when(c == 0)
    def _():
        for _, _, a, b in pair_loads:
            a.start()
            b.start()
        for _, a, b in value_loads:
            a.start()
            b.start()

    @pl.when(c == 1)
    def _():
        for _, a, b in value_loads:
            a.start()
            b.start()
        for _, _, a, b in pair_loads:
            a.start()
            b.start()

    gain_load.start()
    for copy in late_loads:
        copy.start()

    barrier = pltpu.get_barrier_semaphore()
    for dz, dx in OFFSETS:
        pl.semaphore_signal(barrier, inc=1, device_id=(chip_at(dz, dx) * 2 + c, s), device_id_type=MESH)
    for dy, dc in line:
        pl.semaphore_signal(barrier, inc=1, device_id=on_line(dy, dc), device_id_type=MESH)

    def put(source, target, slot, device):
        pltpu.make_async_remote_copy(
            src_ref=source, dst_ref=target, send_sem=send.at[slot], recv_sem=recv.at[slot], device_id=device, device_id_type=MESH
        ).start()

    def arrived(ref, slot):
        pltpu.make_async_copy(ref, ref, recv.at[slot]).wait()

    def gone(ref, slot):
        pltpu.make_async_copy(ref, ref, send.at[slot]).wait()

    for copy in basis_loads:
        copy.wait()

    def pair_stage(out, part=slice(None)):
        for w, r, a, b in pair_loads[part]:
            a.wait()
            b.wait()
            full = presidue[w, r : r + 512, :] + ep[w, r : r + 512, :]
            presidue[w, r : r + 512, :] = full
            store_tiles(out, w * 8 + r // TILE, product(pb[w], *split(full), NT))

    def value_stage(out, part=slice(None)):
        for r, a, b in value_loads[part]:
            a.wait()
            b.wait()
            full = vresidue[r : r + 256, :] + ev[r : r + 256, :]
            vresidue[r : r + 256, :] = full
            store_tiles(out, r // TILE, product(vb[...], *split(full), NT))

    def spread_gain(core):
        gain_load.wait()
        for w in range(2):
            for t in range(8):
                g_own[w, t : t + 1, :] = gg[w : w + 1, t * TILE : (t + 1) * TILE]
        put(g_own.at[1 - core], g_pair, GAIN_PAIR, partner)

    def sum_over_plane(index, pay, rs, res, rows, first=None, second=None):
        slot = 2 * index
        for k, (dz, dx) in enumerate(OFFSETS):
            other = chip_at(dz, dx)
            put(pay.at[pl.ds(pl.multiple_of(other * rows, 8), rows)], rs.at[k], slot, (other * 2 + c, s))
        if first is not None:
            first()
        arrived(rs, slot)
        own = pl.ds(pl.multiple_of(chip * rows, 8), rows)
        total = pay[own, :]
        for k in range(CHIPS - 1):
            total = total + rs[k]
        res[own, :] = total
        for dz, dx in OFFSETS:
            put(res.at[own], res.at[own], slot + 1, (chip_at(dz, dx) * 2 + c, s))
        if second is not None:
            second()
        rest = res.at[pl.ds(0, (CHIPS - 1) * rows)]
        arrived(rest, slot + 1)
        gone(rs, slot)
        gone(rest, slot + 1)

    def sum_over_lines(index, pay, first_in, mid, second_in, res, first, second):
        slot = 2 * index
        half = mid.shape[1]

        def exchange(source, target, along_x, slot):
            for k, step in enumerate((2, 1, 3)):
                for part in range(2):
                    other = chip_at(0, step) if along_x[part] else chip_at(step, 0)
                    put(source[part], target.at[part, k], slot, (other * 2 + c, s))

        def combine(own, pieces):
            return (own + pieces[0]) + (pieces[1] + pieces[2])

        exchange([pay.at[pl.ds(0, half)], pay.at[pl.ds(half, half)]], first_in, (True, False), slot)
        first()
        arrived(first_in, slot)
        for part in range(2):
            mid[part] = combine(pay[part * half : (part + 1) * half, :], first_in[part])
        exchange([mid.at[0], mid.at[1]], second_in, (False, True), slot + 1)
        second()
        arrived(second_in, slot + 1)
        for part in range(2):
            res[part * half : (part + 1) * half, :] = combine(mid[part], second_in[part])
        gone(first_in, slot)
        gone(second_in, slot + 1)

    def transposed(factor, out):
        high, low = split(factor)
        high, low = high.astype(f32), low.astype(f32)
        out[...] = jnp.concatenate([high, high, low], axis=0).T.astype(bf16)

    def right_stack(right):
        high, low = split(right * (1.0 / N_DP))
        return jnp.concatenate([high, low, high], axis=0)

    def rounds(core, left_bufs, right_bufs, count, right_tiles, bases, mats, turned):
        left_pay, left_rs, left_res, left_rows = left_bufs
        right_pay, right_in, right_mid, right_next, right_res = right_bufs
        state = {}

        def lefts(ref):
            return [load_tiles(ref, w * 8, 8) for w in range(count)]

        def rights(ref):
            return [load_tiles(ref, w * right_tiles, right_tiles) for w in range(count)]

        def first_wait():
            if core == 0:
                put(presidue, p_other, BULK, partner)
            else:
                put(vresidue, v_other, BULK, partner)
            state["inverse"] = inverse_factors([gram(b) for b in bases()])

        def gains():
            arrived(g_pair, GAIN_PAIR)
            gone(g_pair, GAIN_PAIR)
            g_send[...] = g_own[core] + g_pair[...]

        def chip_sums():
            if core == 0:
                arrived(v_other, BULK)
                gone(p_other, BULK)
                for r in range(0, D, 128):
                    vh[r : r + 128, :], vlow[r : r + 128, :] = split(vresidue[r : r + 128, :] + v_other[r : r + 128, :])
            else:
                arrived(p_other, BULK)
                gone(v_other, BULK)
                for w in range(2):
                    for r in range(0, D, 256):
                        ph[w, r : r + 256, :], plow[w, r : r + 256, :] = split(presidue[w, r : r + 256, :] + p_other[w, r : r + 256, :])
            gains()

        def spread_gains():
            for k, (dz, dx) in enumerate(OFFSETS):
                put(g_send, g_in.at[k], GAIN_ALL, (chip_at(dz, dx) * 2 + c, s))

        def gain_means():
            arrived(g_in, GAIN_ALL)
            gone(g_in, GAIN_ALL)
            total = g_send[...]
            for k in range(CHIPS - 1):
                total = total + g_in[k]
            g_mean[core] = total / N_DP
            put(g_mean.at[core], g_mean.at[core], GAIN_MEAN, partner)

        for step in range(2):
            last = step == 1
            sum_over_plane(2 * step, left_pay[step], left_rs[step], left_res[step], left_rows, state.pop("overlap", first_wait), None if last else chip_sums)
            left = [whiten(i, a) for i, a in zip(state["inverse"], lefts(left_res[step]))]
            for w, a in enumerate(left):
                store_tiles(right_pay[step], w * right_tiles, product(a, *mats(w), NN))

            def factor_left():
                state["inverse"] = inverse_factors([gram(a) for a in left])
                if last:
                    for w, (i, a) in enumerate(zip(state["inverse"], left)):
                        hat = whiten(i, a)
                        if core == 0:
                            lhv[...] = hat
                        else:
                            lhp[w] = hat
                else:
                    spread_gains()

            def after():
                if last:
                    if core == 0:
                        put(lhv, lhv, LEFT, partner)
                        transposed(lhv[...], ltv)
                        arrived(lhp, LEFT)
                        gone(lhv, LEFT)
                        for w in range(2):
                            transposed(lhp[w], ltp.at[w])
                    else:
                        put(lhp, lhp, LEFT, partner)
                        for w in range(2):
                            transposed(lhp[w], ltp.at[w])
                        arrived(lhv, LEFT)
                        gone(lhp, LEFT)
                        transposed(lhv[...], ltv)
                else:
                    gain_means()
                    for r in range(0, D, 256):
                        at = slice(r, r + 256)
                        if core == 0:
                            vth[:, at] = vh[at, :].T
                            vtlow[:, at] = vlow[at, :].T
                        else:
                            for w in range(2):
                                pth[w, :, at] = ph[w, at, :].T
                                ptlow[w, :, at] = plow[w, at, :].T

            sum_over_lines(2 * step + 1, right_pay[step], right_in[step], right_mid[step], right_next[step], right_res[step], factor_left, after)
            right = [whiten(i, a) for i, a in zip(state["inverse"], rights(right_res[step]))]
            if not last:
                for w, a in enumerate(right):
                    store_tiles(left_pay[1], w * 8, product(a, *turned(w), NN))

                def factor_right():
                    state["inverse"] = inverse_factors([gram(a) for a in right])

                state["overlap"] = factor_right
        return right

    def value_approx():
        stack = right_stack(rv[...])
        for r in range(0, D, 256):
            term = lax.dot_general(ltv[r : r + 256, :], stack, NN, preferred_element_type=f32)
            vresidue[r : r + 256, :] = vresidue[r : r + 256, :] - term
        vfactor[...] = rv[...]

    def pair_approx():
        for w in range(2):
            stack = right_stack(rp[w])
            for r in range(0, D, 512):
                term = lax.dot_general(ltp[w, r : r + 512, :], stack, NN, preferred_element_type=f32)
                presidue[w, r : r + 512, :] = presidue[w, r : r + 512, :] - term
            pfactor[w] = rp[w]

    def squares(terms):
        total = jnp.zeros((8, TILE), f32)
        for term in terms:
            term = term * term
            for r in range(0, term.shape[0], 8):
                for t in range(0, term.shape[1], TILE):
                    total = total + term[r : r + 8, t : t + TILE]
        return total

    def send_part(core, rights):
        part[...] = squares(rights) / (N_DP * N_DP) + squares([g_mean[core]])
        for k, (dy, dc) in enumerate(line):
            put(part, totals.at[k], TOTAL, on_line(dy, dc))

    @pl.when(c == 0)
    def _():
        pair_stage(pl_pay.at[0])
        value_stage(v_own, slice(0, 2))
        pl.semaphore_wait(barrier, len(OFFSETS) + len(line))
        put(pl_pay.at[0], p_in, PRODUCT, partner)
        spread_gain(0)
        value_stage(v_own, slice(2, 4))
        arrived(v_in, PRODUCT)
        v_pay[0] = v_own[...] + v_in[...]
        gone(p_in, PRODUCT)
        bufs = [v_pay.at[0], v_pay.at[1]], [v_rs.at[0], v_rs.at[1]], [v_res.at[0], v_res.at[1]], 16
        more = [[ref.at[i] for i in range(2)] for ref in (vr_pay, vr_in, vr_mid, vr_next, vr_res)]
        (right,) = rounds(0, bufs, more, 1, 8, lambda: [vb[...]], lambda w: (vh[...], vlow[...]), lambda w: (vth[...], vtlow[...]))
        rv[...] = right
        put(rv, rv, RIGHT, partner)
        send_part(0, [right])
        value_approx()
        arrived(rp, RIGHT)
        pair_approx()
        gone(rv, RIGHT)

    @pl.when(c == 1)
    def _():
        value_stage(v_own)
        pair_stage(p_own, slice(0, 2))
        pl.semaphore_wait(barrier, len(OFFSETS) + len(line))
        put(v_own, v_in, PRODUCT, partner)
        spread_gain(1)
        pair_stage(p_own, slice(2, 4))
        arrived(p_in, PRODUCT)
        pl_pay[0] = p_own[...] + p_in[...]
        gone(v_in, PRODUCT)
        bufs = [pl_pay.at[0], pl_pay.at[1]], [pl_rs.at[0], pl_rs.at[1]], [pl_res.at[0], pl_res.at[1]], 32
        more = [[ref.at[i] for i in range(2)] for ref in (pr_pay, pr_in, pr_mid, pr_next, pr_res)]
        right = rounds(1, bufs, more, 2, 2, lambda: [pb[0], pb[1]], lambda w: (ph[w], plow[w]), lambda w: (pth[w], ptlow[w]))
        for w in range(2):
            rp[w] = right[w]
        put(rp, rp, RIGHT, partner)
        send_part(1, right)
        pair_approx()
        arrived(rv, RIGHT)
        value_approx()
        gone(rp, RIGHT)

    for copy in late_loads:
        copy.wait()
    arrived(g_mean.at[0], GAIN_MEAN)
    gone(g_mean.at[0], GAIN_MEAN)
    rows = pl.ds(pl.multiple_of(d * R, R), R)
    vterm = lax.dot_general(ltv[rows, :], right_stack(rv[...]), NN, preferred_element_type=f32)
    pterms = [lax.dot_general(ltp[w, rows, :], right_stack(rp[w]), NN, preferred_element_type=f32) for w in range(2)]
    rv[...] = vterm
    for w in range(2):
        rp[w] = pterms[w]
    arrived(totals, TOTAL)
    gone(totals, TOTAL)
    total = part[...]
    for k in range(len(line)):
        total = total + totals[k]
    total = jnp.sum(jnp.sum(total, axis=0, keepdims=True), axis=1, keepdims=True)
    entries = SECTIONS * (2 * D * QK + D * D + 2 * D)
    scale = 1.0 / jnp.sqrt(total / entries + 1e-06)
    velocity = momentum_rate * vm[...] + scale * rv[...]
    vvel[...] = velocity
    vparams[...] = vw[...] - step_rate * velocity
    for w in range(2):
        velocity = momentum_rate * pm[w] + scale * rp[w]
        pvel[w] = velocity
        pparams[w] = pw[w] - step_rate * velocity
        for t in range(8):
            at = slice(t * TILE, (t + 1) * TILE)
            gparams[w : w + 1, at] = gn[w : w + 1, at] - step_rate * scale * g_mean[w, t : t + 1, :]


def write_out(*refs):
    count = len(refs) // 2
    sems = refs[-1]
    copies = [pltpu.make_async_copy(refs[i], refs[count + i], sems.at[i]) for i in (6, 5, 0, 1, 2, 3, 4, 7, 8)]
    for copy in copies:
        copy.start()
    for copy in copies:
        copy.wait()


def local(
    pair_grads, value_grads, pair_errors, value_errors, pair_basis, value_basis,
    pair_moment, value_moment, pair_weights, value_weights, gain_grads, norm_gains,
):
    any_space = pl.BlockSpec(memory_space=pltpu.HBM)
    vmem = pl.BlockSpec(memory_space=pltpu.VMEM)

    def shape(*dims):
        return jax.ShapeDtypeStruct(dims, f32)

    def scratch(*dims, dtype=f32):
        return pltpu.VMEM(dims, dtype)

    out = pl.pallas_call(
        kernel,
        name="power_rounds",
        out_shape=(
            shape(2, R, QK), shape(R, D), shape(2, R, QK), shape(R, D), shape(2, D),
            shape(2, D, QK), shape(D, D), shape(2, R, QK), shape(R, D),
        ),
        in_specs=[any_space] * 12,
        out_specs=(vmem,) * 9,
        scratch_shapes=[
            scratch(2, D, QK), scratch(D, D), scratch(2, R, QK), scratch(R, D),
            scratch(2, R, QK), scratch(R, D), scratch(2, R, QK), scratch(R, D), scratch(2, D), scratch(2, D),
            scratch(512, TILE), scratch(256, TILE), scratch(512, TILE), scratch(256, TILE),
            scratch(2, D, QK), scratch(D, D),
            scratch(2, D, QK, dtype=bf16), scratch(2, D, QK, dtype=bf16), scratch(D, D, dtype=bf16), scratch(D, D, dtype=bf16),
            scratch(2, QK, D, dtype=bf16), scratch(2, QK, D, dtype=bf16), scratch(D, D, dtype=bf16), scratch(D, D, dtype=bf16),
            scratch(2, 256, TILE), scratch(2, 15, 16, TILE), scratch(2, 256, TILE),
            scratch(2, 512, TILE), scratch(2, 15, 32, TILE), scratch(2, 512, TILE),
            scratch(2, 256, TILE), scratch(2, 2, 3, 128, TILE), scratch(2, 2, 128, TILE), scratch(2, 2, 3, 128, TILE), scratch(2, 256, TILE),
            scratch(2, 128, TILE), scratch(2, 2, 3, 64, TILE), scratch(2, 2, 64, TILE), scratch(2, 2, 3, 64, TILE), scratch(2, 128, TILE),
            scratch(2, 8, TILE), scratch(8, TILE), scratch(8, TILE), scratch(15, 8, TILE), scratch(2, 8, TILE),
            scratch(R, D), scratch(2, R, D), scratch(R, D), scratch(2, R, QK),
            scratch(D, 3 * R, dtype=bf16), scratch(2, D, 3 * R, dtype=bf16),
            scratch(8, TILE), scratch(7, 8, TILE),
            pltpu.SemaphoreType.DMA((24,)), pltpu.SemaphoreType.DMA((16,)), pltpu.SemaphoreType.DMA((16,)),
        ],
        compiler_params=pltpu.CompilerParams(collective_id=0, has_side_effects=True, vmem_limit_bytes=36 * 1024 * 1024),
    )(*(pltpu.with_memory_space_constraint(a, pltpu.HBM) for a in (
        pair_grads[0, 0], value_grads[0, 0], pair_errors[0, 0], value_errors[0, 0], pair_basis[0], value_basis[0],
        pair_moment[0], value_moment[0], pair_weights[0], value_weights[0], gain_grads[0, 0], norm_gains[0],
    )))
    out = pl.pallas_call(
        write_out,
        name="write_out",
        out_shape=tuple(jax.ShapeDtypeStruct(a.shape, f32) for a in out),
        in_specs=[vmem] * 9,
        out_specs=(pl.BlockSpec(memory_space=pltpu.HBM),) * 9,
        scratch_shapes=[pltpu.SemaphoreType.DMA((9,))],
        compiler_params=pltpu.CompilerParams(vmem_limit_bytes=16 * 1024 * 1024),
    )(*out)
    pparams, vparams, pvel, vvel, gparams, presidue, vresidue, pfactor, vfactor = out
    return (
        pparams[None], vparams[None], pvel[None], vvel[None], gparams[None],
        presidue[None, None], vresidue[None, None], pfactor[None], vfactor[None],
    )


def solution(mesh):
    in_specs = (
        P("dp", "section", None, None, None),
        P("dp", "section", None, None),
        P("dp", "section", None, None, None),
        P("dp", "section", None, None),
        P("section", None, None, None),
        P("section", None, None),
        P("section", None, "dp", None),
        P("section", "dp", None),
        P("section", None, "dp", None),
        P("section", "dp", None),
        P("dp", "section", None, None),
        P("section", None, None),
    )
    out_specs = (
        P("section", None, "dp", None),
        P("section", "dp", None),
        P("section", None, "dp", None),
        P("section", "dp", None),
        P("section", None, None),
        P("dp", "section", None, None, None),
        P("dp", "section", None, None),
        P("section", None, None, None),
        P("section", None, None),
    )
    return jax.shard_map(local, mesh=mesh, in_specs=in_specs, out_specs=out_specs, check_vma=False)
```

```python
import jax
import jax.numpy as jnp
from jax import lax
from jax.experimental import pallas as pl
from jax.experimental.pallas import tpu as pltpu
from jax.sharding import PartitionSpec as P

MESH = pl.DeviceIdType.MESH
f32, bf16 = jnp.float32, jnp.bfloat16
NN = (((1,), (0,)), ((), ()))
NT = (((1,), (1,)), ((), ()))
highest = lax.Precision.HIGHEST

D, QK, R = 1024, 256, 32
N_DP, SECTIONS = 32, 4
SIDE = 4
CHIPS = SIDE * SIDE
TILE = 128
momentum_rate = 0.9
step_rate = 0.3

OFFSETS = ((2, 2), (2, 1), (2, 3), (1, 2), (3, 2), (0, 2), (2, 0), (1, 1), (1, 3), (3, 1), (3, 3), (0, 1), (0, 3), (1, 0), (3, 0))

PRODUCT, BULK, GAIN_PAIR, GAIN_ALL, GAIN_MEAN, LEFT, RIGHT, TOTAL = range(8, 16)


def split(a):
    high = a.astype(bf16)
    return high, (a - high.astype(f32)).astype(bf16)


def gram(a):
    return lax.dot_general(a, a, NT, precision=highest, preferred_element_type=f32)


def whiten(inverse, a):
    wh, wl = split(inverse)
    ah, al = split(a)
    left = jnp.concatenate([wh.astype(f32), wl.astype(f32), wh.astype(f32)], axis=1).astype(bf16)
    return lax.dot_general(left, jnp.concatenate([ah, ah, al], axis=0), NN, preferred_element_type=f32)


def inverse_factors(grams):
    row = lax.broadcasted_iota(jnp.int32, (R, 2 * R), 0)
    col = lax.broadcasted_iota(jnp.int32, (R, 2 * R), 1)
    eye = (row[:, :R] == col[:, :R]).astype(f32)

    def step(k, carry):
        out = []
        for both, pivots in carry:
            pivot_row = jnp.sum(jnp.where(row == k, both, 0.0), axis=0, keepdims=True)
            column = jnp.sum(jnp.where(col == k, both, 0.0), axis=1, keepdims=True)
            pivot = jnp.sum(jnp.where(col[:1] == k, pivot_row, 0.0), axis=1, keepdims=True)
            pivots = jnp.where(row[:, :1] == k, pivot, pivots)
            times = jnp.where(row[:, :1] > k, column / pivot, 0.0)
            out.append((both - times * pivot_row, pivots))
        return tuple(out)

    start = tuple((jnp.concatenate([g, eye], axis=1), jnp.zeros((R, 1), f32)) for g in grams)
    done = lax.fori_loop(0, R, step, start)
    return [both[:, R:] / jnp.sqrt(pivots) for both, pivots in done]


def load_tiles(ref, first, tiles):
    return jnp.concatenate([ref[(first + t) * R : (first + t + 1) * R, :] for t in range(tiles)], axis=1)


def store_tiles(ref, first, value):
    for t in range(value.shape[1] // TILE):
        ref[(first + t) * R : (first + t + 1) * R, :] = value[:, t * TILE : (t + 1) * TILE]


def product(factor, high, low, dims):
    both = jnp.concatenate(split(factor), axis=0)
    out = lax.dot_general(both, high, dims, preferred_element_type=f32)
    out = out + lax.dot_general(both, low, dims, preferred_element_type=f32)
    return out[:R] + out[R:]


def kernel(
    pg, vg, pe, ve, pbasis, vbasis, pmoment, vmoment, pweights, vweights, ggrads, gnorm,
    pparams, vparams, pvel, vvel, gparams, presidue, vresidue, pfactor, vfactor,
    ep, ev, pb, vb, pm, vm, pw, vw, gg, gn,
    p_own, v_own, p_in, v_in, p_other, v_other, ph, plow, vh, vlow, pth, ptlow, vth, vtlow,
    v_pay, v_rs, v_res, pl_pay, pl_rs, pl_res,
    vr_pay, vr_in, vr_mid, vr_next, vr_res, pr_pay, pr_in, pr_mid, pr_next, pr_res,
    g_own, g_pair, g_send, g_in, g_mean,
    lhv, lhp, rv, rp, ltv, ltp, part, totals,
    load, send, recv,
):
    d = lax.axis_index("dp")
    s = lax.axis_index("section")
    c = lax.rem(d, 2)
    chip = lax.div(d, 2)
    z, x = lax.div(chip, SIDE), lax.rem(chip, SIDE)
    zs = [lax.rem(z + step, SIDE) * SIDE for step in range(SIDE)]
    xs = [lax.rem(x + step, SIDE) for step in range(SIDE)]
    chips = {(dz, dx): zs[dz] + xs[dx] for dz in range(SIDE) for dx in range(SIDE)}

    def chip_at(dz, dx):
        return chips[dz, dx]

    partner = (chip * 2 + 1 - c, s)
    line = tuple((dy, dc) for dy in (2, 1, 3, 0) for dc in (0, 1) if dy or dc)

    def on_line(dy, dc):
        return (chip * 2 + lax.rem(c + dc, 2), lax.rem(s + dy, SECTIONS))

    loads = []

    def start_load(source, target):
        copy = pltpu.make_async_copy(source, target, load.at[len(loads)])
        loads.append(copy)
        return copy

    basis_loads = [start_load(pbasis, pb), start_load(vbasis, vb)]
    pair_loads = [
        (w, r, start_load(pg.at[w, pl.ds(r, 512)], presidue.at[w, pl.ds(r, 512)]), start_load(pe.at[w, pl.ds(r, 512)], ep.at[w, pl.ds(r, 512)]))
        for w in range(2)
        for r in range(0, D, 512)
    ]
    value_loads = [
        (r, start_load(vg.at[pl.ds(r, 256)], vresidue.at[pl.ds(r, 256)]), start_load(ve.at[pl.ds(r, 256)], ev.at[pl.ds(r, 256)]))
        for r in range(0, D, 256)
    ]
    gain_load = start_load(ggrads, gg)
    late_loads = [start_load(pmoment, pm), start_load(vmoment, vm), start_load(pweights, pw), start_load(vweights, vw), start_load(gnorm, gn)]

    for copy in basis_loads:
        copy.start()

    @pl.when(c == 0)
    def _():
        for _, _, a, b in pair_loads:
            a.start()
            b.start()
        for _, a, b in value_loads:
            a.start()
            b.start()

    @pl.when(c == 1)
    def _():
        for _, a, b in value_loads:
            a.start()
            b.start()
        for _, _, a, b in pair_loads:
            a.start()
            b.start()

    gain_load.start()
    for copy in late_loads:
        copy.start()

    barrier = pltpu.get_barrier_semaphore()
    for dz, dx in OFFSETS:
        pl.semaphore_signal(barrier, inc=1, device_id=(chip_at(dz, dx) * 2 + c, s), device_id_type=MESH)
    for dy, dc in line:
        pl.semaphore_signal(barrier, inc=1, device_id=on_line(dy, dc), device_id_type=MESH)

    def put(source, target, slot, device):
        pltpu.make_async_remote_copy(
            src_ref=source, dst_ref=target, send_sem=send.at[slot], recv_sem=recv.at[slot], device_id=device, device_id_type=MESH
        ).start()

    def arrived(ref, slot):
        pltpu.make_async_copy(ref, ref, recv.at[slot]).wait()

    def gone(ref, slot):
        pltpu.make_async_copy(ref, ref, send.at[slot]).wait()

    for copy in basis_loads:
        copy.wait()

    def pair_stage(out, part=slice(None)):
        for w, r, a, b in pair_loads[part]:
            a.wait()
            b.wait()
            full = presidue[w, r : r + 512, :] + ep[w, r : r + 512, :]
            presidue[w, r : r + 512, :] = full
            store_tiles(out, w * 8 + r // TILE, product(pb[w], *split(full), NT))

    def value_stage(out, part=slice(None)):
        for r, a, b in value_loads[part]:
            a.wait()
            b.wait()
            full = vresidue[r : r + 256, :] + ev[r : r + 256, :]
            vresidue[r : r + 256, :] = full
            store_tiles(out, r // TILE, product(vb[...], *split(full), NT))

    def spread_gain(core):
        gain_load.wait()
        for w in range(2):
            for t in range(8):
                g_own[w, t : t + 1, :] = gg[w : w + 1, t * TILE : (t + 1) * TILE]
        put(g_own.at[1 - core], g_pair, GAIN_PAIR, partner)

    def sum_over_plane(index, pay, rs, res, rows, first=None, second=None):
        slot = 2 * index
        for k, (dz, dx) in enumerate(OFFSETS):
            other = chip_at(dz, dx)
            put(pay.at[pl.ds(pl.multiple_of(other * rows, 8), rows)], rs.at[k], slot, (other * 2 + c, s))
        if first is not None:
            first()
        arrived(rs, slot)
        own = pl.ds(pl.multiple_of(chip * rows, 8), rows)
        total = pay[own, :]
        for k in range(CHIPS - 1):
            total = total + rs[k]
        res[own, :] = total
        for dz, dx in OFFSETS:
            put(res.at[own], res.at[own], slot + 1, (chip_at(dz, dx) * 2 + c, s))
        if second is not None:
            second()
        rest = res.at[pl.ds(0, (CHIPS - 1) * rows)]
        arrived(rest, slot + 1)
        gone(rs, slot)
        gone(rest, slot + 1)

    def sum_over_lines(index, pay, first_in, mid, second_in, res, first, second):
        slot = 2 * index
        half = mid.shape[1]

        def exchange(source, target, along_x, slot):
            for k, step in enumerate((2, 1, 3)):
                for part in range(2):
                    other = chip_at(0, step) if along_x[part] else chip_at(step, 0)
                    put(source[part], target.at[part, k], slot, (other * 2 + c, s))

        def combine(own, pieces):
            return (own + pieces[0]) + (pieces[1] + pieces[2])

        exchange([pay.at[pl.ds(0, half)], pay.at[pl.ds(half, half)]], first_in, (True, False), slot)
        first()
        arrived(first_in, slot)
        for part in range(2):
            mid[part] = combine(pay[part * half : (part + 1) * half, :], first_in[part])
        exchange([mid.at[0], mid.at[1]], second_in, (False, True), slot + 1)
        second()
        arrived(second_in, slot + 1)
        for part in range(2):
            res[part * half : (part + 1) * half, :] = combine(mid[part], second_in[part])
        gone(first_in, slot)
        gone(second_in, slot + 1)

    def transposed(factor, out):
        high, low = split(factor)
        high, low = high.astype(f32), low.astype(f32)
        out[...] = jnp.concatenate([high, high, low], axis=0).T.astype(bf16)

    def right_stack(right):
        high, low = split(right * (1.0 / N_DP))
        return jnp.concatenate([high, low, high], axis=0)

    def rounds(core, left_bufs, right_bufs, count, right_tiles, bases, mats, turned):
        left_pay, left_rs, left_res, left_rows = left_bufs
        right_pay, right_in, right_mid, right_next, right_res = right_bufs
        state = {}

        def lefts(ref):
            return [load_tiles(ref, w * 8, 8) for w in range(count)]

        def rights(ref):
            return [load_tiles(ref, w * right_tiles, right_tiles) for w in range(count)]

        def first_wait():
            if core == 0:
                put(presidue, p_other, BULK, partner)
            else:
                put(vresidue, v_other, BULK, partner)
            state["inverse"] = inverse_factors([gram(b) for b in bases()])

        def gains():
            arrived(g_pair, GAIN_PAIR)
            gone(g_pair, GAIN_PAIR)
            g_send[...] = g_own[core] + g_pair[...]

        def chip_sums():
            if core == 0:
                arrived(v_other, BULK)
                gone(p_other, BULK)
                for r in range(0, D, 128):
                    vh[r : r + 128, :], vlow[r : r + 128, :] = split(vresidue[r : r + 128, :] + v_other[r : r + 128, :])
            else:
                arrived(p_other, BULK)
                gone(v_other, BULK)
                for w in range(2):
                    for r in range(0, D, 256):
                        ph[w, r : r + 256, :], plow[w, r : r + 256, :] = split(presidue[w, r : r + 256, :] + p_other[w, r : r + 256, :])
            gains()

        def spread_gains():
            for k, (dz, dx) in enumerate(OFFSETS):
                put(g_send, g_in.at[k], GAIN_ALL, (chip_at(dz, dx) * 2 + c, s))

        def gain_means():
            arrived(g_in, GAIN_ALL)
            gone(g_in, GAIN_ALL)
            total = g_send[...]
            for k in range(CHIPS - 1):
                total = total + g_in[k]
            g_mean[core] = total / N_DP
            put(g_mean.at[core], g_mean.at[core], GAIN_MEAN, partner)

        for step in range(2):
            last = step == 1
            sum_over_plane(2 * step, left_pay[step], left_rs[step], left_res[step], left_rows, state.pop("overlap", first_wait), None if last else chip_sums)
            left = [whiten(i, a) for i, a in zip(state["inverse"], lefts(left_res[step]))]
            for w, a in enumerate(left):
                store_tiles(right_pay[step], w * right_tiles, product(a, *mats(w), NN))

            def factor_left():
                state["inverse"] = inverse_factors([gram(a) for a in left])
                if last:
                    for w, (i, a) in enumerate(zip(state["inverse"], left)):
                        hat = whiten(i, a)
                        if core == 0:
                            lhv[...] = hat
                        else:
                            lhp[w] = hat
                else:
                    spread_gains()

            def after():
                if last:
                    if core == 0:
                        put(lhv, lhv, LEFT, partner)
                        transposed(lhv[...], ltv)
                        arrived(lhp, LEFT)
                        gone(lhv, LEFT)
                        for w in range(2):
                            transposed(lhp[w], ltp.at[w])
                    else:
                        put(lhp, lhp, LEFT, partner)
                        for w in range(2):
                            transposed(lhp[w], ltp.at[w])
                        arrived(lhv, LEFT)
                        gone(lhp, LEFT)
                        transposed(lhv[...], ltv)
                else:
                    gain_means()
                    for r in range(0, D, 256):
                        at = slice(r, r + 256)
                        if core == 0:
                            vth[:, at] = vh[at, :].T
                            vtlow[:, at] = vlow[at, :].T
                        else:
                            for w in range(2):
                                pth[w, :, at] = ph[w, at, :].T
                                ptlow[w, :, at] = plow[w, at, :].T

            sum_over_lines(2 * step + 1, right_pay[step], right_in[step], right_mid[step], right_next[step], right_res[step], factor_left, after)
            right = [whiten(i, a) for i, a in zip(state["inverse"], rights(right_res[step]))]
            if not last:
                for w, a in enumerate(right):
                    store_tiles(left_pay[1], w * 8, product(a, *turned(w), NN))

                def factor_right():
                    state["inverse"] = inverse_factors([gram(a) for a in right])

                state["overlap"] = factor_right
        return right

    def value_approx():
        stack = right_stack(rv[...])
        for r in range(0, D, 256):
            term = lax.dot_general(ltv[r : r + 256, :], stack, NN, preferred_element_type=f32)
            vresidue[r : r + 256, :] = vresidue[r : r + 256, :] - term
        vfactor[...] = rv[...]

    def pair_approx():
        for w in range(2):
            stack = right_stack(rp[w])
            for r in range(0, D, 512):
                term = lax.dot_general(ltp[w, r : r + 512, :], stack, NN, preferred_element_type=f32)
                presidue[w, r : r + 512, :] = presidue[w, r : r + 512, :] - term
            pfactor[w] = rp[w]

    def squares(terms):
        total = jnp.zeros((8, TILE), f32)
        for term in terms:
            term = term * term
            for r in range(0, term.shape[0], 8):
                for t in range(0, term.shape[1], TILE):
                    total = total + term[r : r + 8, t : t + TILE]
        return total

    def send_part(core, rights):
        part[...] = squares(rights) / (N_DP * N_DP) + squares([g_mean[core]])
        for k, (dy, dc) in enumerate(line):
            put(part, totals.at[k], TOTAL, on_line(dy, dc))

    @pl.when(c == 0)
    def _():
        pair_stage(pl_pay.at[0])
        value_stage(v_own, slice(0, 2))
        pl.semaphore_wait(barrier, len(OFFSETS) + len(line))
        put(pl_pay.at[0], p_in, PRODUCT, partner)
        spread_gain(0)
        value_stage(v_own, slice(2, 4))
        arrived(v_in, PRODUCT)
        v_pay[0] = v_own[...] + v_in[...]
        gone(p_in, PRODUCT)
        bufs = [v_pay.at[0], v_pay.at[1]], [v_rs.at[0], v_rs.at[1]], [v_res.at[0], v_res.at[1]], 16
        more = [[ref.at[i] for i in range(2)] for ref in (vr_pay, vr_in, vr_mid, vr_next, vr_res)]
        (right,) = rounds(0, bufs, more, 1, 8, lambda: [vb[...]], lambda w: (vh[...], vlow[...]), lambda w: (vth[...], vtlow[...]))
        rv[...] = right
        send_part(0, [right])
        put(rv, rv, RIGHT, partner)
        value_approx()
        arrived(rp, RIGHT)
        pair_approx()
        gone(rv, RIGHT)

    @pl.when(c == 1)
    def _():
        value_stage(v_own)
        pair_stage(p_own, slice(0, 2))
        pl.semaphore_wait(barrier, len(OFFSETS) + len(line))
        put(v_own, v_in, PRODUCT, partner)
        spread_gain(1)
        pair_stage(p_own, slice(2, 4))
        arrived(p_in, PRODUCT)
        pl_pay[0] = p_own[...] + p_in[...]
        gone(v_in, PRODUCT)
        bufs = [pl_pay.at[0], pl_pay.at[1]], [pl_rs.at[0], pl_rs.at[1]], [pl_res.at[0], pl_res.at[1]], 32
        more = [[ref.at[i] for i in range(2)] for ref in (pr_pay, pr_in, pr_mid, pr_next, pr_res)]
        right = rounds(1, bufs, more, 2, 2, lambda: [pb[0], pb[1]], lambda w: (ph[w], plow[w]), lambda w: (pth[w], ptlow[w]))
        for w in range(2):
            rp[w] = right[w]
        send_part(1, right)
        put(rp, rp, RIGHT, partner)
        pair_approx()
        arrived(rv, RIGHT)
        value_approx()
        gone(rp, RIGHT)

    for copy in late_loads:
        copy.wait()
    arrived(g_mean.at[0], GAIN_MEAN)
    gone(g_mean.at[0], GAIN_MEAN)
    rows = pl.ds(pl.multiple_of(d * R, R), R)
    vterm = lax.dot_general(ltv[rows, :], right_stack(rv[...]), NN, preferred_element_type=f32)
    pterms = [lax.dot_general(ltp[w, rows, :], right_stack(rp[w]), NN, preferred_element_type=f32) for w in range(2)]
    rv[...] = vterm
    for w in range(2):
        rp[w] = pterms[w]
    arrived(totals, TOTAL)
    gone(totals, TOTAL)
    total = part[...]
    for k in range(len(line)):
        total = total + totals[k]
    total = jnp.sum(jnp.sum(total, axis=0, keepdims=True), axis=1, keepdims=True)
    entries = SECTIONS * (2 * D * QK + D * D + 2 * D)
    scale = 1.0 / jnp.sqrt(total / entries + 1e-06)
    velocity = momentum_rate * vm[...] + scale * rv[...]
    vvel[...] = velocity
    vparams[...] = vw[...] - step_rate * velocity
    for w in range(2):
        velocity = momentum_rate * pm[w] + scale * rp[w]
        pvel[w] = velocity
        pparams[w] = pw[w] - step_rate * velocity
        for t in range(8):
            at = slice(t * TILE, (t + 1) * TILE)
            gparams[w : w + 1, at] = gn[w : w + 1, at] - step_rate * scale * g_mean[w, t : t + 1, :]


def write_out(*refs):
    count = len(refs) // 2
    sems = refs[-1]
    copies = [pltpu.make_async_copy(refs[i], refs[count + i], sems.at[i]) for i in (6, 5, 0, 1, 2, 3, 4, 7, 8)]
    for copy in copies:
        copy.start()
    for copy in copies:
        copy.wait()


def local(
    pair_grads, value_grads, pair_errors, value_errors, pair_basis, value_basis,
    pair_moment, value_moment, pair_weights, value_weights, gain_grads, norm_gains,
):
    any_space = pl.BlockSpec(memory_space=pltpu.HBM)
    vmem = pl.BlockSpec(memory_space=pltpu.VMEM)

    def shape(*dims):
        return jax.ShapeDtypeStruct(dims, f32)

    def scratch(*dims, dtype=f32):
        return pltpu.VMEM(dims, dtype)

    out = pl.pallas_call(
        kernel,
        name="power_rounds",
        out_shape=(
            shape(2, R, QK), shape(R, D), shape(2, R, QK), shape(R, D), shape(2, D),
            shape(2, D, QK), shape(D, D), shape(2, R, QK), shape(R, D),
        ),
        in_specs=[any_space] * 12,
        out_specs=(vmem,) * 9,
        scratch_shapes=[
            scratch(2, D, QK), scratch(D, D), scratch(2, R, QK), scratch(R, D),
            scratch(2, R, QK), scratch(R, D), scratch(2, R, QK), scratch(R, D), scratch(2, D), scratch(2, D),
            scratch(512, TILE), scratch(256, TILE), scratch(512, TILE), scratch(256, TILE),
            scratch(2, D, QK), scratch(D, D),
            scratch(2, D, QK, dtype=bf16), scratch(2, D, QK, dtype=bf16), scratch(D, D, dtype=bf16), scratch(D, D, dtype=bf16),
            scratch(2, QK, D, dtype=bf16), scratch(2, QK, D, dtype=bf16), scratch(D, D, dtype=bf16), scratch(D, D, dtype=bf16),
            scratch(2, 256, TILE), scratch(2, 15, 16, TILE), scratch(2, 256, TILE),
            scratch(2, 512, TILE), scratch(2, 15, 32, TILE), scratch(2, 512, TILE),
            scratch(2, 256, TILE), scratch(2, 2, 3, 128, TILE), scratch(2, 2, 128, TILE), scratch(2, 2, 3, 128, TILE), scratch(2, 256, TILE),
            scratch(2, 128, TILE), scratch(2, 2, 3, 64, TILE), scratch(2, 2, 64, TILE), scratch(2, 2, 3, 64, TILE), scratch(2, 128, TILE),
            scratch(2, 8, TILE), scratch(8, TILE), scratch(8, TILE), scratch(15, 8, TILE), scratch(2, 8, TILE),
            scratch(R, D), scratch(2, R, D), scratch(R, D), scratch(2, R, QK),
            scratch(D, 3 * R, dtype=bf16), scratch(2, D, 3 * R, dtype=bf16),
            scratch(8, TILE), scratch(7, 8, TILE),
            pltpu.SemaphoreType.DMA((24,)), pltpu.SemaphoreType.DMA((16,)), pltpu.SemaphoreType.DMA((16,)),
        ],
        compiler_params=pltpu.CompilerParams(collective_id=0, has_side_effects=True, vmem_limit_bytes=36 * 1024 * 1024),
    )(*(pltpu.with_memory_space_constraint(a, pltpu.HBM) for a in (
        pair_grads[0, 0], value_grads[0, 0], pair_errors[0, 0], value_errors[0, 0], pair_basis[0], value_basis[0],
        pair_moment[0], value_moment[0], pair_weights[0], value_weights[0], gain_grads[0, 0], norm_gains[0],
    )))
    out = pl.pallas_call(
        write_out,
        name="write_out",
        out_shape=tuple(jax.ShapeDtypeStruct(a.shape, f32) for a in out),
        in_specs=[vmem] * 9,
        out_specs=(pl.BlockSpec(memory_space=pltpu.HBM),) * 9,
        scratch_shapes=[pltpu.SemaphoreType.DMA((9,))],
        compiler_params=pltpu.CompilerParams(vmem_limit_bytes=16 * 1024 * 1024),
    )(*out)
    pparams, vparams, pvel, vvel, gparams, presidue, vresidue, pfactor, vfactor = out
    return (
        pparams[None], vparams[None], pvel[None], vvel[None], gparams[None],
        presidue[None, None], vresidue[None, None], pfactor[None], vfactor[None],
    )


def solution(mesh):
    in_specs = (
        P("dp", "section", None, None, None),
        P("dp", "section", None, None),
        P("dp", "section", None, None, None),
        P("dp", "section", None, None),
        P("section", None, None, None),
        P("section", None, None),
        P("section", None, "dp", None),
        P("section", "dp", None),
        P("section", None, "dp", None),
        P("section", "dp", None),
        P("dp", "section", None, None),
        P("section", None, None),
    )
    out_specs = (
        P("section", None, "dp", None),
        P("section", "dp", None),
        P("section", None, "dp", None),
        P("section", "dp", None),
        P("section", None, None),
        P("dp", "section", None, None, None),
        P("dp", "section", None, None),
        P("section", None, None, None),
        P("section", None, None),
    )
    return jax.shard_map(local, mesh=mesh, in_specs=in_specs, out_specs=out_specs, check_vma=False)
```
